256 devices in a mesh: tok: 8 (over z_lo, x), feat: 32 (over z_hi, y, core).
Axes of the slice: x: 4, y: 4, z: 8 (z_hi: 4, z_lo: 2; z = z_hi * 2 + z_lo), core: 2. Of those that a mesh axis runs over, the one named last changes fastest.
Arguments:
- features: bfloat16 [8192, 16384], P('tok', 'feat'), may hold values from -6 to 6
- kernel: bfloat16 [16384, 256], P('feat'), may hold values from -6 to 6
- mask: int32 [16384, 256], P('feat'), may hold values 0 or 1
- inverse: float32 [16384, 16384], P('tok', 'feat'), may hold values from -1 to 2, as said below
- penalty: float32 [3], replicated, may hold values from 0.3 to 3
Outputs:
- pruned: bfloat16 [16384, 256], P('feat')
- applied: bfloat16 [256, 8192], P('feat', 'tok')
The draws below stay inside these ranges and needn't reach their ends.
Inputs may be any that keep to these rules, and one draw needn't show every extreme that they name: inverse is exactly symmetric.
All inputs are finite; a program needn't handle non-finite values. No bound on the sum of `mask` on one device may be relied on, other than what follows from the above.
Results may differ from the reference program's by a relative error of at most 0.0048.
Values sent between devices are 32-bit elements; how exact they have to be, the bound alone decides.
No kernel may reach another device: no remote copies, remote signals or barrier semaphores. Data moves between devices by JAX's collectives and lax.ppermute only.
A program may use at most 64 MiB of HBM per device.

```python
import math
import jax
import jax.numpy as jnp
from jax import lax

D = 16384
R = 256
ITERS = 3
TOKENS = 8192


def draw_inverse(key, part):
    first = jax.random.fold_in(key, 11)
    second = jax.random.fold_in(key, 23)
    spread = 0.5 / math.sqrt(D)
    base = jax.random.truncated_normal(first, -4.0, 4.0, (D, D), jnp.float32) * spread
    sym = (base + base.T) * 0.5
    diag_vals = jax.random.uniform(second, (D,), jnp.float32, 0.8, 1.4)
    rows = lax.broadcasted_iota(jnp.int32, (D, D), 0)
    cols = lax.broadcasted_iota(jnp.int32, (D, D), 1)
    return jnp.where(rows == cols, diag_vals[:, None], 0.0) + sym


def with_ends(result, key, smallest, top_value):
    spot = [jax.random.randint(jax.random.fold_in(key, axis), (), 0, length) for axis, length in enumerate(result.shape)]
    widest = result.shape.index(max(result.shape))
    beside = spot[:widest] + [(spot[widest] + 1) % result.shape[widest]] + spot[widest + 1:]
    return result.at[tuple(spot)].set(smallest).at[tuple(beside)].set(top_value)


def shard_levels(own_key, shape, cuts, smallest, largest):
    level, own = 1.0, jax.random.fold_in(own_key, 6)
    for position, blocks in cuts:
        draws = jnp.exp(jax.random.uniform(jax.random.fold_in(own, position), (blocks,), jnp.float32, smallest / len(cuts), largest / len(cuts)))
        level = level * jnp.repeat(draws, shape[position] // blocks).reshape([-1 if axis == position else 1 for axis in range(len(shape))])
    return level


def noise(key, extent, scale, limit, cuts=(), kind=jnp.bfloat16):
    drawn = scale * jax.random.normal(key, extent, jnp.float32)
    if cuts:
        drawn = drawn * shard_levels(key, extent, cuts, -0.22, 0.18)
    return jnp.clip(drawn, -limit, limit).astype(kind)


def setup_inputs(seed: int = 0) -> dict:
    key_list = jax.random.split(jax.random.key(seed), 6)
    return {
        "features": noise(key_list[0], (TOKENS, D), 1.0, 6.0, ((0, 8), (1, 32))),
        "kernel": noise(key_list[1], (D, R), 1.0, 6.0, ((0, 32),)),
        "mask": with_ends((jax.random.randint(key_list[2], (D, R), 0, 2) < 1).astype(jnp.int32), jax.random.fold_in(key_list[2], 1), 0, 1),
        "inverse": draw_inverse(jax.random.fold_in(key_list[5], 71), 0),
        "penalty": jnp.clip(jnp.exp(jax.random.uniform(key_list[4], (ITERS,), jnp.float32, math.log(0.3), math.log(3.0))), 0.3, 3.0),
    }


def reference(features, kernel, mask, inverse, penalty):
    scale = 1.0 / math.sqrt(D)
    targets = (jnp.dot(features, kernel, preferred_element_type=jnp.float32) * scale).astype(jnp.bfloat16)
    sides = jnp.dot(features.T, targets, preferred_element_type=jnp.float32) * (math.sqrt(D) / TOKENS)
    keeps = mask.astype(jnp.float32)
    slab = keeps * kernel.astype(jnp.float32)
    dual = jnp.zeros(slab.shape, jnp.float32)
    for step in range(ITERS):
        rhs = sides + penalty[step] * (slab - dual)
        solved = jnp.dot(inverse, rhs, precision=lax.Precision.HIGHEST, preferred_element_type=jnp.float32)
        slab = keeps * (solved + dual)
        dual = dual + solved - slab
    pruned = slab.astype(jnp.bfloat16)
    applied = (jnp.dot(pruned.T, features.T, preferred_element_type=jnp.float32) * scale).astype(jnp.bfloat16)
    return (pruned, applied)
```

```python
import math

import jax
import jax.numpy as jnp
from jax import lax
from jax.sharding import Mesh, PartitionSpec as P


SWAP = [(0, 1), (1, 0)]


def swap(value):
    return lax.ppermute(value, "core", SWAP)


def spread(value, axis):
    count = lax.axis_size(axis)
    pieces = value.reshape((count, value.shape[0] // count) + value.shape[1:])
    return jnp.sum(lax.all_to_all(pieces, axis, 0, 0), axis=0)


def collect(value, axis):
    count = lax.axis_size(axis)
    copies = jnp.broadcast_to(value[None], (count,) + value.shape)
    pieces = lax.all_to_all(copies, axis, 0, 0)
    return pieces.reshape((count * value.shape[0],) + value.shape[1:])


def halves(value):
    high = lax.reduce_precision(value, 8, 7)
    return high.astype(jnp.bfloat16), (value - high).astype(jnp.bfloat16)


def per_device(features, kernel, mask, inverse, penalty):
    n_tok = lax.axis_size("tok")
    n_chip = lax.axis_size("chip")
    block, rows = kernel.shape
    half = rows // 2
    group = rows // (2 * n_chip)
    width = block * n_chip * 2
    tokens = features.shape[0] * n_tok
    scale = 1.0 / math.sqrt(width)
    core = lax.axis_index("core")
    tok = lax.axis_index("tok")

    place = lax.broadcasted_iota(jnp.int32, (rows, rows), 1)
    source = lax.broadcasted_iota(jnp.int32, (rows, rows), 0)
    owner = jnp.where(place < half, core, 1 - core)
    local = place % half
    wanted = (2 * (local // group) + owner) * group + local % group
    order = (source == wanted).astype(jnp.bfloat16)
    weights = jnp.dot(kernel, order, preferred_element_type=jnp.float32)
    keeps_all = jnp.dot(
        mask.astype(jnp.bfloat16), order, preferred_element_type=jnp.float32
    )

    partial_value = jnp.dot(
        features, weights.astype(jnp.bfloat16), preferred_element_type=jnp.float32
    )
    pair = partial_value[:, :half] + swap(partial_value[:, half:])
    summed = spread(pair, "chip")
    targets = (collect(summed, "chip") * scale).astype(jnp.bfloat16)

    other_features = (swap(features.astype(jnp.float32)) * 2.0).astype(jnp.bfloat16)
    side_own = lax.dot_general(
        features, targets, (((0,), (0,)), ((), ())), preferred_element_type=jnp.float32
    )
    side_other = lax.dot_general(
        other_features, targets, (((0,), (0,)), ((), ())), preferred_element_type=jnp.float32
    )
    side_part = jnp.concatenate([side_own, side_other * 0.5], axis=0)
    sides = spread(side_part, "tok") * (math.sqrt(width) / tokens)

    start_all = keeps_all * weights
    moved = swap(jnp.stack([start_all[:, half:], keeps_all[:, half:]]))
    start = jnp.concatenate([start_all[:, :half], moved[0]], axis=0)
    keeps_chip = jnp.concatenate([keeps_all[:, :half], moved[1]], axis=0)
    piece = 2 * block // n_tok
    slab = lax.dynamic_slice_in_dim(start, tok * piece, piece, 0)
    keeps = lax.dynamic_slice_in_dim(keeps_chip, tok * piece, piece, 0)
    dual = jnp.zeros(slab.shape, jnp.float32)

    full = jnp.concatenate([inverse, swap(inverse)], axis=1)
    high, low = halves(full)

    per_row = n_chip // n_tok
    moves = []
    for t in range(n_tok):
        for chip in range(n_chip):
            for c in range(2):
                first = (t * n_chip + chip) * 2 + c
                to_chip = t * per_row + chip // n_tok
                to_tok = (chip % n_tok) ^ (n_tok // 2 * c)
                moves.append((first, (to_tok * n_chip + to_chip) * 2 + c))

    steps = penalty.shape[0]
    for step in range(steps):
        rhs = sides + penalty[step] * (slab - dual)
        column = collect(rhs, "tok")
        col_high, col_low = halves(column)
        both = jnp.dot(
            high,
            jnp.concatenate([col_high, col_low], axis=1),
            preferred_element_type=jnp.float32,
        )
        rest = jnp.dot(low, col_high, preferred_element_type=jnp.float32)
        part = both[:, :half] + (both[:, half:] + rest)
        solved = lax.ppermute(spread(part, "chip"), ("tok", "chip", "core"), moves)
        total = solved + dual
        slab = keeps * total
        dual = dual + solved - slab

    total_chip = collect(total, "tok")
    pruned_chip = (keeps_chip * total_chip).astype(jnp.bfloat16)
    term = lax.dot_general(
        pruned_chip[:block], features, (((0,), (1,)), ((), ())),
        preferred_element_type=jnp.float32,
    ) + 0.5 * lax.dot_general(
        pruned_chip[block:], other_features, (((0,), (1,)), ((), ())),
        preferred_element_type=jnp.float32,
    )
    applied = (spread(term, "chip") * scale).astype(jnp.bfloat16)

    crossed = (swap(total_chip[block:]) * keeps_all[:, half:]).astype(jnp.bfloat16)
    mixed = jnp.concatenate([pruned_chip[:block], crossed], axis=1)
    pruned = lax.dot_general(
        mixed, order, (((1,), (1,)), ((), ())), preferred_element_type=jnp.float32
    ).astype(jnp.bfloat16)
    return (pruned, applied)


def solution(mesh):
    n_tok, n_feat = mesh.devices.shape
    fine = Mesh(
        mesh.devices.reshape(n_tok, n_feat // 2, 2), ("tok", "chip", "core")
    )
    feat = ("chip", "core")
    return jax.shard_map(
        per_device,
        mesh=fine,
        in_specs=(P("tok", feat), P(feat, None), P(feat, None), P("tok", feat), P()),
        out_specs=(P(feat, None), P(feat, "tok")),
        check_vma=False,
    )
```

```python
import math

import jax
import jax.numpy as jnp
from jax import lax
from jax.sharding import Mesh, PartitionSpec as P


SWAP = [(0, 1), (1, 0)]


def swap(value):
    return lax.ppermute(value, "core", SWAP)


def exchange(pieces, axis):
    return lax.all_to_all(pieces, axis, 0, 0)


def copies(value, axis):
    return jnp.broadcast_to(value[None], (lax.axis_size(axis),) + value.shape)


def cut(value, count):
    rows, width = value.shape
    return jnp.swapaxes(value.reshape(rows, count, width // count), 0, 1)


def join(pieces):
    count, rows, width = pieces.shape
    return jnp.swapaxes(pieces, 0, 1).reshape(rows, count * width)


def halves(value):
    high = lax.reduce_precision(value, 8, 7)
    return high.astype(jnp.bfloat16), (value - high).astype(jnp.bfloat16)


def dot(left, right, left_dim, right_dim):
    return lax.dot_general(
        left, right, (((left_dim,), (right_dim,)), ((), ())),
        preferred_element_type=jnp.float32,
    )


def per_device(features, kernel, mask, inverse, penalty):
    n_tok = lax.axis_size("tok")
    n_chip = lax.axis_size("chip")
    block, rows = kernel.shape
    half = rows // 2
    group = rows // (2 * n_chip)
    width = block * n_chip * 2
    tokens = features.shape[0] * n_tok
    scale = 1.0 / math.sqrt(width)
    core = lax.axis_index("core")
    tok = lax.axis_index("tok")

    place = lax.broadcasted_iota(jnp.int32, (rows, rows), 0)
    source = lax.broadcasted_iota(jnp.int32, (rows, rows), 1)
    owner = jnp.where(place < half, core, 1 - core)
    local = place % half
    wanted = (2 * (local // group) + owner) * group + local % group
    order = (source == wanted).astype(jnp.bfloat16)
    weights = dot(order, kernel, 1, 1)
    keeps_all = dot(order, mask.astype(jnp.bfloat16), 1, 1)

    partial_value = dot(weights.astype(jnp.bfloat16), features, 1, 1)
    pair = partial_value[:half] + swap(partial_value[half:])
    pair = pair.reshape(n_chip, half // n_chip, -1)
    start_all = keeps_all * weights
    moved = swap(jnp.stack([start_all[half:], keeps_all[half:]]))
    start = jnp.concatenate([start_all[:half], moved[0]], axis=1)
    keeps_chip = jnp.concatenate([keeps_all[:half], moved[1]], axis=1)

    own_halves = halves(inverse)
    pieces, own_halves = lax.optimization_barrier((exchange(pair, "chip"), own_halves))
    summed = jnp.sum(pieces, axis=0)
    targets = exchange(copies(summed, "chip"), "chip").reshape(half, -1)
    high, low = [
        jnp.concatenate(pair, axis=1) for pair in zip(own_halves, halves(swap(inverse)))
    ]
    targets, high, low, start, keeps_chip = lax.optimization_barrier(
        (targets, high, low, start, keeps_chip)
    )
    targets = (targets * scale).astype(jnp.bfloat16)

    other_features = (swap(features.astype(jnp.float32)) * 2.0).astype(jnp.bfloat16)
    side_part = jnp.concatenate(
        [dot(targets, features, 1, 0), dot(targets, other_features, 1, 0) * 0.5], axis=1
    )

    per_row = n_chip // n_tok
    moves = []
    for t in range(n_tok):
        for chip in range(n_chip):
            for c in range(2):
                first = (t * n_chip + chip) * 2 + c
                to_chip = t * per_row + chip // n_tok
                to_tok = (chip % n_tok) ^ (n_tok // 2 * c)
                moves.append((first, (to_tok * n_chip + to_chip) * 2 + c))
    back = [(last, first) for first, last in moves]
    everyone = ("tok", "chip", "core")

    piece = 2 * block // n_tok
    keeps_row = lax.dynamic_slice_in_dim(keeps_chip, tok * piece, piece, 1)
    keeps_row = lax.ppermute(keeps_row, everyone, back)
    sides = exchange(cut(side_part, n_tok), "tok")
    sides, keeps_row = lax.optimization_barrier((sides, keeps_row))
    sides = jnp.sum(sides, axis=0) * (math.sqrt(width) / tokens)

    chip = lax.axis_index("chip")
    share = chip % per_row
    inside = tok == chip // per_row
    sign = 2.0 * keeps_chip - 1.0
    first_half, second_half = slice(0, block), slice(block, 2 * block)

    def to_row(value):
        blocks = []
        for i in range(2 * per_row):
            here = inside & (share == i // 2)
            use = jnp.where(core == i % 2, value[:, first_half], value[:, second_half])
            blocks.append(jnp.where(here, use, 0.0))
        return jnp.concatenate(blocks, axis=1)

    def product(column, contract):
        col_high, col_low = halves(column)
        both = dot(jnp.concatenate([col_high, col_low], axis=0), high, 1, contract)
        rest = dot(col_high, low, 1, contract)
        return both[:half] + (both[half:] + rest)

    def gather(value, axis):
        return exchange(copies(value, axis), axis)

    sides_chip = join(gather(sides, "tok"))
    dual = jnp.zeros(start.shape, jnp.float32)
    rhs = sides_chip + penalty[0] * (start - dual)
    part = product(rhs, 1) + to_row(dual + sign * sides_chip / penalty[1])
    mixed = jnp.sum(exchange(cut(part, n_chip), "chip"), axis=0)
    rhs = gather((2.0 * keeps_row - 1.0) * (penalty[1] * mixed), "chip")
    count = n_chip // (2 * per_row)
    near = lax.dynamic_slice_in_dim(rhs, (2 * share + core) * count, count, 0)
    far = lax.dynamic_slice_in_dim(rhs, (2 * share + 1 - core) * count, count, 0)
    total_chip = sign * (jnp.concatenate([join(near), join(far)], axis=1) - sides_chip)
    total_chip = total_chip / penalty[1]
    dual = total_chip - keeps_chip * total_chip
    part = product(join(rhs), 0) + jnp.where(inside, dual, 0.0)
    total = jnp.sum(exchange(cut(part, n_tok), "tok"), axis=0)
    total_chip = join(gather(total, "tok"))
    slab = keeps_chip * total_chip
    dual = total_chip - slab
    rhs = sides_chip + penalty[2] * (slab - dual)
    part = product(rhs, 1) + to_row(dual)
    total = jnp.sum(exchange(cut(part, n_chip), "chip"), axis=0)
    total = lax.ppermute(total, everyone, moves)
    total_chip = join(gather(total, "tok"))
    pruned_chip = (keeps_chip * total_chip).astype(jnp.bfloat16)
    term = dot(pruned_chip[:, :block], features, 1, 1)
    term = term + 0.5 * dot(pruned_chip[:, block:], other_features, 1, 1)
    term = term.reshape(n_chip, half // n_chip, -1)
    applied = (jnp.sum(exchange(term, "chip"), axis=0) * scale).astype(jnp.bfloat16)

    crossed = (swap(total_chip[:, block:]) * keeps_all[half:]).astype(jnp.bfloat16)
    mixed = jnp.concatenate([pruned_chip[:, :block], crossed], axis=0)
    pruned = dot(mixed, order, 0, 0).astype(jnp.bfloat16)
    return (pruned, applied)


def solution(mesh):
    n_tok, n_feat = mesh.devices.shape
    fine = Mesh(
        mesh.devices.reshape(n_tok, n_feat // 2, 2), ("tok", "chip", "core")
    )
    feat = ("chip", "core")
    return jax.shard_map(
        per_device,
        mesh=fine,
        in_specs=(P("tok", feat), P(feat, None), P(feat, None), P("tok", feat), P()),
        out_specs=(P(feat, None), P(feat, "tok")),
        check_vma=False,
    )
```

```python
import math

import jax
import jax.numpy as jnp
from jax import lax
from jax.sharding import Mesh, PartitionSpec as P


SWAP = [(0, 1), (1, 0)]


def swap(value):
    return lax.ppermute(value, "core", SWAP)


def exchange(pieces, axis):
    return lax.all_to_all(pieces, axis, 0, 0)


def copies(value, axis):
    return jnp.broadcast_to(value[None], (lax.axis_size(axis),) + value.shape)


def gather(value, axis):
    return exchange(copies(value, axis), axis)


def sum_chips(pieces):
    return jnp.sum(exchange(pieces, ("y", "z")), axis=0)


def sum_chips_staged(pieces):
    pieces = pieces.reshape((lax.axis_size("y"), -1) + pieces.shape[1:])
    pieces = jnp.sum(exchange(pieces, "y"), axis=0)
    return jnp.sum(exchange(pieces, "z"), axis=0)


def gather_chips(value):
    return gather(value, ("y", "z"))


def cut(value, count):
    rows, width = value.shape
    return jnp.swapaxes(value.reshape(rows, count, width // count), 0, 1)


def join(pieces):
    count, rows, width = pieces.shape
    return jnp.swapaxes(pieces, 0, 1).reshape(rows, count * width)


def halves(value):
    high = lax.reduce_precision(value, 8, 7)
    return high.astype(jnp.bfloat16), (value - high).astype(jnp.bfloat16)


def dot(left, right, left_dim, right_dim):
    return lax.dot_general(
        left, right, (((left_dim,), (right_dim,)), ((), ())),
        preferred_element_type=jnp.float32,
    )


def per_device(features, kernel, mask, inverse, penalty):
    n_tok = lax.axis_size("tok")
    n_y = lax.axis_size("y")
    n_z = lax.axis_size("z")
    n_chip = n_z * n_y
    block, rows = kernel.shape
    half = rows // 2
    group = rows // (2 * n_chip)
    width = block * n_chip * 2
    tokens = features.shape[0] * n_tok
    scale = 1.0 / math.sqrt(width)
    core = lax.axis_index("core")
    tok = lax.axis_index("tok")

    place = lax.broadcasted_iota(jnp.int32, (rows, rows), 0)
    source = lax.broadcasted_iota(jnp.int32, (rows, rows), 1)
    owner = jnp.where(place < half, core, 1 - core)
    local = place % half
    number = local // group
    chip = number % n_z * n_y + number // n_z
    wanted = (2 * chip + owner) * group + local % group
    order = (source == wanted).astype(jnp.bfloat16)
    weights = dot(order, kernel, 1, 1)
    keeps_all = dot(order, mask.astype(jnp.bfloat16), 1, 1)

    partial_value = dot(weights.astype(jnp.bfloat16), features, 1, 1)
    pair = partial_value[:half] + swap(partial_value[half:])
    pair = pair.reshape(n_chip, half // n_chip, -1)
    pair, features, weights, keeps_all, inverse = lax.optimization_barrier(
        (pair, features, weights, keeps_all, inverse)
    )
    start_all = keeps_all * weights
    moved = swap(jnp.stack([start_all[half:], keeps_all[half:]]))
    start = jnp.concatenate([start_all[:half], moved[0]], axis=1)
    keeps_chip = jnp.concatenate([keeps_all[:half], moved[1]], axis=1)

    per_row = n_chip // n_tok
    subs = n_tok // 2
    everyone = ("tok", "z", "y", "core")
    moves, keeps_moves = [], []
    for t in range(n_tok):
        for chip in range(n_chip):
            for c in range(2):
                first = (t * n_chip + chip) * 2 + c
                number = chip % n_y * n_z + chip // n_y
                to_chip = t * per_row + number // n_tok
                to_tok = (number % n_tok) ^ (subs * c)
                moves.append((first, (to_tok * n_chip + to_chip) * 2 + c))
                feat = chip * 2 + c
                to_tok = feat // (2 * per_row)
                number = feat % (2 * per_row) * subs + t % subs
                to_chip = number % n_z * n_y + number // n_z
                keeps_moves.append((first, (to_tok * n_chip + to_chip) * 2 + t // subs))

    piece = block // subs
    keeps_row = jnp.where(tok // subs == core, keeps_all[:half], keeps_all[half:])
    keeps_row = lax.dynamic_slice_in_dim(keeps_row, tok % subs * piece, piece, 1)

    own_halves = halves(inverse)
    summed, own_halves = lax.optimization_barrier((sum_chips(pair), own_halves))
    targets = gather_chips(summed).reshape(half, -1)
    high, low = [
        jnp.concatenate(pair, axis=1) for pair in zip(own_halves, halves(swap(inverse)))
    ]
    targets, high, low, start, keeps_chip, keeps_row = lax.optimization_barrier(
        (targets, high, low, start, keeps_chip, keeps_row)
    )
    keeps_row = lax.ppermute(keeps_row, everyone, keeps_moves)
    targets = (targets * scale).astype(jnp.bfloat16)

    other_features = (swap(features.astype(jnp.float32)) * 2.0).astype(jnp.bfloat16)
    side_part = jnp.concatenate(
        [dot(targets, features, 1, 0), dot(targets, other_features, 1, 0) * 0.5], axis=1
    )

    sides = exchange(cut(side_part, n_tok), "tok")
    sides, keeps_row = lax.optimization_barrier((sides, keeps_row))
    sides = jnp.sum(sides, axis=0) * (math.sqrt(width) / tokens)

    chip = lax.axis_index(("z", "y"))
    share = chip % per_row
    inside = tok == chip // per_row
    sign = 2.0 * keeps_chip - 1.0
    first_half, second_half = slice(0, block), slice(block, 2 * block)

    def to_row(value):
        blocks = []
        for i in range(2 * per_row):
            here = inside & (share == i // 2)
            use = jnp.where(core == i % 2, value[:, first_half], value[:, second_half])
            blocks.append(jnp.where(here, use, 0.0))
        return jnp.concatenate(blocks, axis=1)

    def product(column, contract):
        col_high, col_low = halves(column)
        both = dot(jnp.concatenate([col_high, col_low], axis=0), high, 1, contract)
        rest = dot(col_high, low, 1, contract)
        return both[:half] + (both[half:] + rest)

    sides_chip = join(gather(sides, "tok"))
    dual = jnp.zeros(start.shape, jnp.float32)
    rhs = sides_chip + penalty[0] * (start - dual)
    part = product(rhs, 1) + to_row(dual + sign * sides_chip / penalty[1])
    mixed = sum_chips_staged(cut(part, n_chip))
    rhs = gather_chips((2.0 * keeps_row - 1.0) * (penalty[1] * mixed))
    count = n_chip // (2 * per_row)
    near = lax.dynamic_slice_in_dim(rhs, (2 * share + core) * count, count, 0)
    far = lax.dynamic_slice_in_dim(rhs, (2 * share + 1 - core) * count, count, 0)
    total_chip = sign * (jnp.concatenate([join(near), join(far)], axis=1) - sides_chip)
    total_chip = total_chip / penalty[1]
    dual = total_chip - keeps_chip * total_chip
    part = product(join(rhs), 0) + jnp.where(inside, dual, 0.0)
    total = jnp.sum(exchange(cut(part, n_tok), "tok"), axis=0)
    total_chip = join(gather(total, "tok"))
    slab = keeps_chip * total_chip
    dual = total_chip - slab
    rhs = sides_chip + penalty[2] * (slab - dual)
    part = product(rhs, 1) + to_row(dual)
    total = sum_chips_staged(cut(part, n_chip))
    total = lax.ppermute(total, everyone, moves)
    total_chip = join(gather(total, "tok"))
    pruned_chip = (keeps_chip * total_chip).astype(jnp.bfloat16)
    term = dot(pruned_chip[:, :block], features, 1, 1)
    term = term + 0.5 * dot(pruned_chip[:, block:], other_features, 1, 1)
    term = term.reshape(n_chip, half // n_chip, -1)
    term, total_chip = lax.optimization_barrier((term, total_chip))
    applied = (sum_chips(term) * scale).astype(jnp.bfloat16)

    crossed = (swap(total_chip[:, block:]) * keeps_all[half:]).astype(jnp.bfloat16)
    mixed = jnp.concatenate([pruned_chip[:, :block], crossed], axis=0)
    pruned = dot(mixed, order, 0, 0).astype(jnp.bfloat16)
    return (pruned, applied)


def solution(mesh):
    n_tok, n_feat = mesh.devices.shape
    n_y = math.isqrt(n_feat // 2)
    fine = Mesh(
        mesh.devices.reshape(n_tok, n_feat // (2 * n_y), n_y, 2), ("tok", "z", "y", "core")
    )
    feat = ("z", "y", "core")
    return jax.shard_map(
        per_device,
        mesh=fine,
        in_specs=(P("tok", feat), P(feat, None), P(feat, None), P("tok", feat), P()),
        out_specs=(P(feat, None), P(feat, "tok")),
        check_vma=False,
    )
```

```python
import math

import jax
import jax.numpy as jnp
from jax import lax
from jax.sharding import Mesh, PartitionSpec as P


SWAP = [(0, 1), (1, 0)]


def swap(value):
    return lax.ppermute(value, "core", SWAP)


def exchange(pieces, axis):
    return lax.all_to_all(pieces, axis, 0, 0)


def copies(value, axis):
    return jnp.broadcast_to(value[None], (lax.axis_size(axis),) + value.shape)


def gather(value, axis):
    return exchange(copies(value, axis), axis)


def sum_chips(pieces):
    return jnp.sum(exchange(pieces, ("y", "z")), axis=0)


def sum_chips_staged(pieces):
    pieces = pieces.reshape((lax.axis_size("y"), -1) + pieces.shape[1:])
    pieces = jnp.sum(exchange(pieces, "y"), axis=0)
    return jnp.sum(exchange(pieces, "z"), axis=0)


def gather_chips(value):
    return gather(value, ("y", "z"))


def gather_chips_staged(value):
    return gather(gather(value, "z"), "y").reshape((-1,) + value.shape)


def cut(value, count):
    rows, width = value.shape
    return jnp.swapaxes(value.reshape(rows, count, width // count), 0, 1)


def join(pieces):
    count, rows, width = pieces.shape
    return jnp.swapaxes(pieces, 0, 1).reshape(rows, count * width)


def halves(value):
    high = lax.reduce_precision(value, 8, 7)
    return high.astype(jnp.bfloat16), (value - high).astype(jnp.bfloat16)


def dot(left, right, left_dim, right_dim):
    return lax.dot_general(
        left, right, (((left_dim,), (right_dim,)), ((), ())),
        preferred_element_type=jnp.float32,
    )


def per_device(features, kernel, mask, inverse, penalty):
    n_tok = lax.axis_size("tok")
    n_y = lax.axis_size("y")
    n_z = lax.axis_size("z")
    n_chip = n_z * n_y
    block, rows = kernel.shape
    half = rows // 2
    group = rows // (2 * n_chip)
    width = block * n_chip * 2
    tokens = features.shape[0] * n_tok
    scale = 1.0 / math.sqrt(width)
    core = lax.axis_index("core")
    tok = lax.axis_index("tok")

    place = lax.broadcasted_iota(jnp.int32, (rows, rows), 0)
    source = lax.broadcasted_iota(jnp.int32, (rows, rows), 1)
    owner = jnp.where(place < half, core, 1 - core)
    local = place % half
    number = local // group
    chip = number % n_z * n_y + number // n_z
    wanted = (2 * chip + owner) * group + local % group
    order = (source == wanted).astype(jnp.bfloat16)
    weights = dot(order, kernel, 1, 1)
    keeps_all = dot(order, mask.astype(jnp.bfloat16), 1, 1)

    partial_value = dot(weights.astype(jnp.bfloat16), features, 1, 1)
    pair = partial_value[:half] + swap(partial_value[half:])
    pair = pair.reshape(n_chip, half // n_chip, -1)
    pair, features, weights, keeps_all, inverse = lax.optimization_barrier(
        (pair, features, weights, keeps_all, inverse)
    )
    start_all = keeps_all * weights
    moved = swap(jnp.stack([start_all[half:], keeps_all[half:]]))
    start = jnp.concatenate([start_all[:half], moved[0]], axis=1)
    keeps_chip = jnp.concatenate([keeps_all[:half], moved[1]], axis=1)

    per_row = n_chip // n_tok
    subs = n_tok // 2
    everyone = ("tok", "z", "y", "core")
    moves, keeps_moves = [], []
    for t in range(n_tok):
        for chip in range(n_chip):
            for c in range(2):
                first = (t * n_chip + chip) * 2 + c
                number = chip % n_y * n_z + chip // n_y
                to_chip = t * per_row + number // n_tok
                to_tok = (number % n_tok) ^ (subs * c)
                moves.append((first, (to_tok * n_chip + to_chip) * 2 + c))
                feat = chip * 2 + c
                to_tok = feat // (2 * per_row)
                number = feat % (2 * per_row) * subs + t % subs
                to_chip = number % n_z * n_y + number // n_z
                keeps_moves.append((first, (to_tok * n_chip + to_chip) * 2 + t // subs))

    piece = block // subs
    keeps_row = jnp.where(tok // subs == core, keeps_all[:half], keeps_all[half:])
    keeps_row = lax.dynamic_slice_in_dim(keeps_row, tok % subs * piece, piece, 1)

    own_halves = halves(inverse)
    summed, own_halves = lax.optimization_barrier((sum_chips(pair), own_halves))
    targets = gather_chips(summed).reshape(half, -1)
    high, low = [
        jnp.concatenate(pair, axis=1) for pair in zip(own_halves, halves(swap(inverse)))
    ]
    targets, high, low, start, keeps_chip, keeps_row = lax.optimization_barrier(
        (targets, high, low, start, keeps_chip, keeps_row)
    )
    keeps_row = lax.ppermute(keeps_row, everyone, keeps_moves)
    targets = (targets * scale).astype(jnp.bfloat16)

    other_features = (swap(features.astype(jnp.float32)) * 2.0).astype(jnp.bfloat16)
    side_part = jnp.concatenate(
        [dot(targets, features, 1, 0), dot(targets, other_features, 1, 0) * 0.5], axis=1
    )

    sides = exchange(cut(side_part, n_tok), "tok")
    sides, keeps_row = lax.optimization_barrier((sides, keeps_row))
    sides = jnp.sum(sides, axis=0) * (math.sqrt(width) / tokens)

    chip = lax.axis_index(("z", "y"))
    share = chip % per_row
    inside = tok == chip // per_row
    sign = 2.0 * keeps_chip - 1.0
    first_half, second_half = slice(0, block), slice(block, 2 * block)

    def to_row(value):
        blocks = []
        for i in range(2 * per_row):
            here = inside & (share == i // 2)
            use = jnp.where(core == i % 2, value[:, first_half], value[:, second_half])
            blocks.append(jnp.where(here, use, 0.0))
        return jnp.concatenate(blocks, axis=1)

    def product(column, contract):
        col_high, col_low = halves(column)
        both = dot(jnp.concatenate([col_high, col_low], axis=0), high, 1, contract)
        rest = dot(col_high, low, 1, contract)
        return both[:half] + (both[half:] + rest)

    sides_chip = join(gather(sides, "tok"))
    dual = jnp.zeros(start.shape, jnp.float32)
    rhs = sides_chip + penalty[0] * (start - dual)
    part = product(rhs, 1) + to_row(dual + sign * sides_chip / penalty[1])
    mixed = sum_chips_staged(cut(part, n_chip))
    rhs = gather_chips_staged((2.0 * keeps_row - 1.0) * (penalty[1] * mixed))
    count = n_chip // (2 * per_row)
    near = lax.dynamic_slice_in_dim(rhs, (2 * share + core) * count, count, 0)
    far = lax.dynamic_slice_in_dim(rhs, (2 * share + 1 - core) * count, count, 0)
    total_chip = sign * (jnp.concatenate([join(near), join(far)], axis=1) - sides_chip)
    total_chip = total_chip / penalty[1]
    dual = total_chip - keeps_chip * total_chip
    part = product(join(rhs), 0) + jnp.where(inside, dual, 0.0)
    total = jnp.sum(exchange(cut(part, n_tok), "tok"), axis=0)
    total_chip = join(gather(total, "tok"))
    slab = keeps_chip * total_chip
    dual = total_chip - slab
    rhs = sides_chip + penalty[2] * (slab - dual)
    part = product(rhs, 1) + to_row(dual)
    total = sum_chips_staged(cut(part, n_chip))
    total = lax.ppermute(total, everyone, moves)
    total_chip = join(gather(total, "tok"))
    pruned_chip = (keeps_chip * total_chip).astype(jnp.bfloat16)
    term = dot(pruned_chip[:, :block], features, 1, 1)
    term = term + 0.5 * dot(pruned_chip[:, block:], other_features, 1, 1)
    term = term.reshape(n_chip, half // n_chip, -1)
    term, total_chip = lax.optimization_barrier((term, total_chip))
    applied = (sum_chips(term) * scale).astype(jnp.bfloat16)

    crossed = (swap(total_chip[:, block:]) * keeps_all[half:]).astype(jnp.bfloat16)
    mixed = jnp.concatenate([pruned_chip[:, :block], crossed], axis=0)
    pruned = dot(mixed, order, 0, 0).astype(jnp.bfloat16)
    return (pruned, applied)


def solution(mesh):
    n_tok, n_feat = mesh.devices.shape
    n_y = math.isqrt(n_feat // 2)
    fine = Mesh(
        mesh.devices.reshape(n_tok, n_feat // (2 * n_y), n_y, 2), ("tok", "z", "y", "core")
    )
    feat = ("z", "y", "core")
    return jax.shard_map(
        per_device,
        mesh=fine,
        in_specs=(P("tok", feat), P(feat, None), P(feat, None), P("tok", feat), P()),
        out_specs=(P(feat, None), P(feat, "tok")),
        check_vma=False,
    )
```
